32 devices in a mesh: range: 8 (over y, x, core), pulse: 4 (over z).
Axes of the slice: x: 2, y: 2, z: 4, core: 2. Of those that a mesh axis runs over, the one named last changes fastest.
Arguments:
- samples: float32 [8192, 2048], P('range', 'pulse'), may hold values from -100 to 100
- taps: float32 [128], replicated, may hold values from -0.5 to 0.5
- taper: float32 [64], P('pulse'), may hold values from 0.5 to 1.5
Outputs:
- whitened: float32 [8192, 2048], P('range', 'pulse')
The draws below stay inside these ranges and needn't reach their ends.
All inputs are finite; a program needn't handle non-finite values.
Results may differ from the reference program's by a relative error of at most 0.0003.
Values sent between devices are 32-bit elements; how exact they have to be, the bound alone decides.
A program may use at most 64 MiB of HBM per device.

```python
import math
import jax
import jax.numpy as jnp
from jax import lax

RG_DEV = 1024
BINS = 16
CH = 16
TAPS = 128
GATES = 8192
PULSES = 64
N_PULSE = 4


def draw_samples(key, part):
    row_key, chan_key, base_key = jax.random.split(key, 3)
    gate_block = max(RG_DEV // 8, 1)
    total_columns = PULSES * 2 * CH
    gate_scale = jnp.exp(jax.random.uniform(row_key, (GATES // gate_block,), jnp.float32, 0.0, math.log(10.0)))
    gate_scale = jnp.repeat(gate_scale, gate_block)
    chan_scale = jnp.exp(jax.random.uniform(chan_key, (CH,), jnp.float32, 0.0, math.log(10.0)))
    column_scale = jnp.tile(jnp.repeat(chan_scale, 2), PULSES)
    noise = jax.random.truncated_normal(base_key, -4.0, 4.0, (GATES, total_columns), jnp.float32)
    return noise * gate_scale[:, None] * column_scale[None, :] / 10.0


def bell_draw(rng, extent, spread, reach, held_as=jnp.bfloat16):
    array = spread * jax.random.normal(rng, extent, jnp.float32)
    return jnp.clip(array, min=-reach, max=reach).astype(held_as)


def setup_inputs(seed: int = 0) -> dict:
    streams_of = jax.random.split(jax.random.key(seed), 4)
    return {
        "samples": draw_samples(jax.random.fold_in(streams_of[3], 71), 0),
        "taps": bell_draw(streams_of[1], (TAPS,), TAPS ** -0.5, 0.5, jnp.float32),
        "taper": jnp.clip(1.0 + 0.1 * jax.random.normal(streams_of[2], (PULSES,), jnp.float32), 0.5, 1.5),
    }


LOADING = 0.05

def toeplitz(taps, tile_rows):
    tap_count = taps.shape[0]
    padded_taps = jnp.concatenate([taps, jnp.zeros((tile_rows,), taps.dtype)])
    repeated = jnp.tile(padded_taps, tile_rows)[:tile_rows * (tap_count + tile_rows - 1)]
    return repeated.reshape(tile_rows, tap_count + tile_rows - 1)

def doppler_matrix(pulses):
    position = jnp.arange(pulses, dtype=jnp.int32)
    phase_index = position[:, None] * position[None, :] % pulses
    angles = phase_index.astype(jnp.float32) * (2.0 * math.pi / pulses)
    amplitude = 1.0 / math.sqrt(pulses)
    cosine = jnp.cos(angles) * amplitude
    sine_part = jnp.sin(angles) * amplitude
    real_in = jnp.stack([cosine, -sine_part], axis=1)
    imag_in = jnp.stack([sine_part, cosine], axis=1)
    return jnp.stack([real_in, imag_in], axis=1)

def reference(samples, taps, taper):
    tap_count = taps.shape[0]
    half_taps = tap_count // 2
    tile_rows = min(128, RG_DEV)
    padded = jnp.pad(samples, ((half_taps, half_taps), (0, 0)))
    matrix = toeplitz(taps, tile_rows)

    def compress_block(first_row):
        window = lax.dynamic_slice_in_dim(padded, first_row, tile_rows + tap_count - 1, 0)
        return jnp.dot(matrix.astype(jnp.float32), window.astype(jnp.float32), precision=lax.Precision.HIGHEST, preferred_element_type=jnp.float32)
    starts = jnp.arange(GATES // tile_rows, dtype=jnp.int32) * tile_rows
    compressed = lax.map(compress_block, starts).reshape(GATES, PULSES * 2 * CH)
    tapered = compressed * jnp.repeat(taper, 2 * CH)[None, :]
    arranged = tapered.reshape(GATES, PULSES, CH, 2)
    doppler = jnp.einsum('rpca,pabk->rkcb', arranged, doppler_matrix(PULSES), precision=lax.Precision.HIGHEST)
    doppler = doppler.reshape(GATES, N_PULSE, 2 * BINS * CH)
    identity = jnp.eye(2 * BINS * CH, dtype=jnp.float32)

    def whiten(position):
        snapshot = lax.dynamic_index_in_dim(doppler, position, 1, keepdims=False)
        covariance = jnp.dot(snapshot.T.astype(jnp.float32), snapshot.astype(jnp.float32), precision=lax.Precision.HIGHEST, preferred_element_type=jnp.float32) / GATES + LOADING * identity
        factor = jnp.linalg.cholesky(covariance)
        return lax.linalg.triangular_solve(factor, snapshot, left_side=False, lower=True, transpose_a=True)
    whitened = lax.map(whiten, jnp.arange(N_PULSE, dtype=jnp.int32))
    return jnp.transpose(whitened, (1, 0, 2)).reshape(GATES, PULSES * 2 * CH)
```

```python
import functools
import math

import jax
import jax.numpy as jnp
import numpy as np
from jax import lax
from jax.experimental import pallas as pl
from jax.experimental.pallas import tpu as pltpu
from jax.sharding import PartitionSpec as P

LOADING = 0.05


PANEL = 16
LANES = 128
CHUNKS = 4
FEEDS = 2
HIGHEST = lax.Precision.HIGHEST


def split3(x):
    high = x.astype(jnp.bfloat16)
    rest = x - high.astype(jnp.float32)
    middle = rest.astype(jnp.bfloat16)
    low = (rest - middle.astype(jnp.float32)).astype(jnp.bfloat16)
    return high, middle, low


def eliminate_panel(work_ref, first, block):
    last = first + PANEL
    tile = work_ref[first:last, :]
    width = tile.shape[1]
    row = lax.broadcasted_iota(jnp.int32, (PANEL, block), 0)
    columns = [
        jnp.broadcast_to(tile[:, first + c : first + c + 1], (PANEL, block)) for c in range(PANEL)
    ]
    left, right = tile[:, :block], tile[:, block:]
    for r in range(PANEL):
        inverse = lax.rsqrt(columns[r][r : r + 1, :])
        below = jnp.where(row > r, columns[r] * inverse, 0.0)
        for c in range(r + 1, PANEL):
            columns[c] = columns[c] - below * (columns[c][r : r + 1, :] * inverse)
        left_row = left[r : r + 1, :] * inverse
        right_row = right[r : r + 1, :] * inverse
        left = jnp.where(row == r, left_row, left - below * left_row)
        right = jnp.where(row == r, right_row, right - below * right_row)
    tile = jnp.concatenate([left, right], axis=1)
    work_ref[first:last, :] = tile
    if last < block:
        high, middle, low = split3(tile)
        lhs = jnp.concatenate([high, high, middle, middle, high, low], axis=0)[:, :block]
        rhs = jnp.concatenate([high, middle, high, middle, low, high], axis=0)
        update = lax.dot_general(
            lhs, rhs, (((0,), (0,)), ((), ())), preferred_element_type=jnp.float32
        )
        work_ref[last:, :] = work_ref[last:, :] - update[last:, :]


def greet(partners):
    barrier = pltpu.get_barrier_semaphore()
    for axis, target in partners:
        pl.semaphore_signal(
            barrier, inc=1, device_id={axis: target}, device_id_type=pl.DeviceIdType.MESH
        )
    pl.semaphore_wait(barrier, len(partners))


def send(src, dst, send_sem, recv_sem, axis, target):
    copy = pltpu.make_async_remote_copy(
        src_ref=src, dst_ref=dst, send_sem=send_sem, recv_sem=recv_sem,
        device_id={axis: target}, device_id_type=pl.DeviceIdType.MESH,
    )
    copy.start()
    return copy


def slice_rows(rows, ranges):
    return -(-rows // (8 * ranges)) * 8


def stages_of(blocks):
    first = max(blocks // 2, 1)
    return [list(range(first))] + [[b] for b in range(first, blocks)]


def owned_rows(owner, chunk):
    return pl.ds(pl.multiple_of(owner * chunk, 8), chunk)


def scatter_over_range(part_ref, inbox_ref, send_sem, recv_sem):
    me, ranges = lax.axis_index("range"), lax.axis_size("range")
    outs = []
    for shift in range(1, ranges):
        to = lax.rem(me + shift, ranges)
        outs.append(
            send(
                part_ref.at[owned_rows(to, inbox_ref.shape[1])], inbox_ref.at[shift - 1],
                send_sem.at[shift - 1], recv_sem.at[shift - 1], "range", to,
            )
        )
    return outs


def gather_over_range(outs, part_ref, inbox_ref, total_ref, send_sem, recv_sem):
    me, ranges = lax.axis_index("range"), lax.axis_size("range")
    rows = owned_rows(me, inbox_ref.shape[1])
    own = part_ref[rows]
    for shift in range(1, ranges):
        outs[shift - 1].wait_recv()
        own = own + inbox_ref[shift - 1]
    total_ref[rows] = own
    source = total_ref.at[rows]
    return [
        send(
            source, source, send_sem.at[s - 1], recv_sem.at[s - 1],
            "range", lax.rem(me + s, ranges),
        )
        for s in range(1, ranges)
    ]


def dot_nt(x, y):
    return lax.dot_general(
        x, y, (((1,), (1,)), ((), ())), precision=HIGHEST, preferred_element_type=jnp.float32
    )


def gram_rows(stage, snapshot_ref, part_ref):
    block = snapshot_ref.shape[2]
    used = 0
    for number in stage:
        mine = snapshot_ref[number]
        for first in range(0, number + 1, 2):
            blocks = range(first, min(first + 2, number + 1))
            other = jnp.concatenate([snapshot_ref[b] for b in blocks], axis=1)
            gram = lax.dot_general(
                mine, other, (((0,), (0,)), ((), ())), precision=HIGHEST,
                preferred_element_type=jnp.float32,
            )
            for n in range(len(blocks)):
                part_ref[used : used + block, :] = gram[:, n * block : (n + 1) * block]
                used += block
    if part_ref.shape[0] > used:
        part_ref[used:, :] = jnp.zeros((part_ref.shape[0] - used, block), jnp.float32)


def factor_row(
    number, at, last, total_gates, total_ref, snapshot_ref, solved_ref, inverse_ref, work_ref, emit
):
    block = work_ref.shape[0]
    r = lax.broadcasted_iota(jnp.int32, (block, block), 0)
    c = lax.broadcasted_iota(jnp.int32, (block, block), 1)
    piece = snapshot_ref.shape[1] // CHUNKS
    done = number * block

    def total(b):
        return total_ref[at + b * block : at + (b + 1) * block, :] * (1.0 / total_gates)

    diagonal = total(number) + jnp.where(r == c, LOADING, 0.0)
    left = None
    if number:
        row = jnp.concatenate([total(b) for b in range(number)], axis=1)
        left = dot_nt(row, inverse_ref[:done, :done])
        diagonal = diagonal - dot_nt(left, left)
    work_ref[:, :block] = diagonal
    work_ref[:, block:] = jnp.where(r == c, 1.0, 0.0)

    def subtract(part):
        rows = slice(part * piece, (part + 1) * piece)
        before = jnp.concatenate([solved_ref[b, rows] for b in range(number)], axis=1)
        solved_ref[number, rows] = snapshot_ref[number, rows] - dot_nt(before, left)

    waiting = list(range(CHUNKS)) if number else []
    for step, first in enumerate(range(0, block, PANEL)):
        eliminate_panel(work_ref, first, block)
        if waiting and step % 2 == 0:
            subtract(waiting.pop(0))
    while waiting:
        subtract(waiting.pop(0))
    inverse = work_ref[:, block:]
    source_ref = solved_ref if number else snapshot_ref
    for part in range(CHUNKS):
        rows = slice(part * piece, (part + 1) * piece)
        solved_ref[number, rows] = dot_nt(source_ref[number, rows], inverse)
        emit(number, part)
    if not last:
        end = done + block
        if number:
            scaled = jnp.dot(inverse, left, precision=HIGHEST, preferred_element_type=jnp.float32)
            inverse_ref[done:end, :done] = -jnp.dot(
                scaled, inverse_ref[:done, :done], precision=HIGHEST,
                preferred_element_type=jnp.float32,
            )
            inverse_ref[:done, done:end] = jnp.zeros((done, block), jnp.float32)
        inverse_ref[done:end, done:end] = inverse


def quarter_turn(x):
    lane = lax.broadcasted_iota(jnp.int32, x.shape, 1)
    width = x.shape[1]
    return jnp.where(
        lane % 2 == 0, pltpu.roll(x, width - 1, axis=1), -pltpu.roll(x, 1, axis=1)
    )


def doppler_constants(pulses, devices, group):
    bins = pulses // devices
    lane = np.arange(bins * group)
    turn = (lane // group)[None, :] * np.arange(devices)[:, None] % pulses
    angle = turn * (2.0 * math.pi / pulses)
    first = np.arange(bins)
    phase = (first[:, None] * first[None, :] % bins) * (2.0 * math.pi / bins)
    cosine, sine = np.cos(phase), np.sin(phase)
    pair = np.stack(
        [np.stack([cosine, -sine], axis=-1), np.stack([sine, cosine], axis=-1)], axis=1
    ) / math.sqrt(pulses)
    table = np.einsum("paqb,cd->pcaqdb", pair, np.eye(group // 2))
    table = table.reshape(bins * group, bins * group)
    return tuple(np.asarray(v, np.float32) for v in (np.cos(angle), np.sin(angle), table))


def transform_chunk(rows, group, gathered_ref, const_ref, stage_ref, spread_ref):
    devices, _, width = gathered_ref.shape
    count = rows.size
    bins = width // group
    for at in range(0, width, LANES):
        lanes = slice(at, at + LANES)
        parts = [gathered_ref[z, rows, lanes] for z in range(devices)]
        turned = [quarter_turn(x) for x in parts]
        for k in range(devices):
            total = None
            for z in range(devices):
                step = z * k % devices
                for weight, term in (
                    (math.cos(2.0 * math.pi * step / devices), parts[z]),
                    (math.sin(2.0 * math.pi * step / devices), turned[z]),
                ):
                    if abs(weight) < 1e-9:
                        continue
                    sign = 1.0 if weight > 0 else -1.0
                    if abs(abs(weight) - 1.0) > 1e-9:
                        term, sign = term * weight, 1.0
                    if total is None:
                        total = term if sign > 0 else -term
                    else:
                        total = total + term if sign > 0 else total - term
            total = total * const_ref[width + k : width + k + 1, lanes] + quarter_turn(
                total
            ) * const_ref[width + devices + k : width + devices + k + 1, lanes]
            stage_ref[k * count : (k + 1) * count, lanes] = total
    mixed = jnp.dot(
        stage_ref[...], const_ref[:width, :], precision=HIGHEST, preferred_element_type=jnp.float32
    )
    place = lax.broadcasted_iota(jnp.int32, (count, LANES), 1) // group
    for target in range(devices):
        for at in range(0, width, LANES):
            out = None
            for n in range(LANES // group):
                k = target * bins + at // group + n
                low, high = k % devices, k // devices
                source = high * group
                block = source // LANES * LANES
                piece = mixed[low * count : (low + 1) * count, block : block + LANES]
                shift = (n * group - source) % LANES
                if shift:
                    piece = pltpu.roll(piece, shift, axis=1)
                out = piece if out is None else jnp.where(place == n, piece, out)
            spread_ref[target, at // LANES, rows, :] = out


def exchange(
    samples_ref, taps_ref, taper_ref, load, load_const, const_ref, snapshot_ref, low_ref, high_ref,
    padded_ref, outgoing_ref, gathered_ref, stage_ref, spread_ref, group, sems, use_stages
):
    halo_send, halo_recv, in_send, in_recv, back_send, back_recv = sems
    gates, width = samples_ref.shape
    devices, share, _ = gathered_ref.shape
    half = low_ref.shape[0]
    count = share // CHUNKS
    z = lax.axis_index("pulse")
    me, ranges = lax.axis_index("range"), lax.axis_size("range")

    halos = [
        send(
            samples_ref.at[gates - half :], low_ref, halo_send.at[0], halo_recv.at[0],
            "range", lax.rem(me + 1, ranges),
        ),
        send(
            samples_ref.at[:half], high_ref, halo_send.at[1], halo_recv.at[1],
            "range", lax.rem(me + ranges - 1, ranges),
        ),
    ]
    tap_count = taps_ref.shape[1]
    room = -(-(tap_count + count) // LANES) * LANES
    taps = jnp.concatenate(
        [taps_ref[...], jnp.zeros((1, room - tap_count), jnp.float32)], axis=1
    )
    span = count + 2 * half
    band = pltpu.roll(
        jnp.broadcast_to(taps, (count, room)), 0, axis=1, stride=1, stride_axis=0
    )[:, :span]
    pulse = lax.broadcasted_iota(jnp.int32, (1, width), 1) // group
    taper = jnp.zeros((1, width), jnp.float32)
    for p in range(width // group):
        taper = jnp.where(pulse == p, taper_ref[p], taper)
    inner = [
        p for p in range(CHUNKS) if p * count >= half and share - (p + 1) * count >= half
    ]
    outer = [p for p in range(CHUNKS) if p not in inner]
    order = inner + outer
    shifts = sorted(range(1, devices), key=lambda s: abs(2 * s - devices))
    ins = {}
    load.wait()
    for part in order:
        if part == outer[0]:
            for copy in halos:
                copy.wait_recv()
            padded_ref[:half, :] = jnp.where(me > 0, low_ref[...], 0.0)
            padded_ref[half + gates :, :] = jnp.where(me < ranges - 1, high_ref[...], 0.0)
        for shift in shifts + [0]:
            target = lax.rem(z + shift, devices)
            start = pl.multiple_of(target * share + part * count, 8)
            value = taper * jnp.dot(
                band, padded_ref[pl.ds(start, span), :], precision=HIGHEST,
                preferred_element_type=jnp.float32,
            )
            rows = pl.ds(part * count, count)
            if shift == 0:
                gathered_ref[z, rows, :] = value
                continue
            here = outgoing_ref.at[pl.ds(start, count)]
            here[...] = value
            ins[part, shift] = send(
                here, gathered_ref.at[z, rows], in_send.at[shift - 1, part],
                in_recv.at[shift - 1, part], "pulse", target,
            )
    load_const.wait()
    backs = {}
    blocks = width // LANES
    early = len(stages_of(blocks)[0])
    length = share // FEEDS
    later = [(b, n, n * length, length) for b in range(early, blocks) for n in range(FEEDS)]

    def feed():
        if later:
            send_back(*later.pop(0))

    def arrive(stage):
        while later and later[0][0] in stage:
            feed()
        for block in stage:
            for copy in backs[block]:
                copy.wait_recv()

    def send_back(block, part, start, length):
        for shift in shifts:
            target = lax.rem(z + shift, devices)
            home = pl.ds(pl.multiple_of(z * share + start, 8), length)
            backs.setdefault(block, []).append(
                send(
                    spread_ref.at[target, block, pl.ds(start, length)],
                    snapshot_ref.at[block, home],
                    back_send.at[shift - 1, block, part], back_recv.at[shift - 1, block, part],
                    "pulse", target,
                )
            )

    for part in order:
        rows = pl.ds(part * count, count)
        for shift in shifts:
            ins[part, shift].wait_recv()
        transform_chunk(rows, group, gathered_ref, const_ref, stage_ref, spread_ref)
        for block in range(early):
            send_back(block, part, part * count, count)
        home = pl.ds(pl.multiple_of(z * share + part * count, 8), count)
        for block in range(blocks):
            snapshot_ref[block, home, :] = spread_ref[z, block, rows, :]
    feed()
    use_stages(arrive, feed)
    return halos + list(ins.values()) + [copy for b in range(blocks) for copy in backs[b]]


def whole_kernel(
    total_gates, group, samples_ref, taps_ref, taper_ref, given_ref, out_ref,
    snapshot_ref, low_ref, high_ref, padded_ref, outgoing_ref, gathered_ref, stage_ref,
    spread_ref, const_ref, work_ref, solved_ref, inverse_ref, load_sem, const_sem, out_sem, *rest
):
    z, devices = lax.axis_index("pulse"), lax.axis_size("pulse")
    me, ranges = lax.axis_index("range"), lax.axis_size("range")
    gates, width = samples_ref.shape
    blocks, _, block = snapshot_ref.shape
    half = low_ref.shape[0]
    pulse_sems, rest = rest[:6], rest[6:]
    load = pltpu.make_async_copy(samples_ref, padded_ref.at[half : half + gates], load_sem)
    load.start()
    load_const = pltpu.make_async_copy(given_ref, const_ref, const_sem)
    load_const.start()
    greet(
        [("range", lax.rem(me + shift, ranges)) for shift in range(1, ranges)]
        + [("pulse", lax.rem(z + shift, devices)) for shift in range(1, devices)]
    )
    piece = gates // CHUNKS
    written, summed = [], []

    def emit(column, part):
        rows = slice(part * piece, (part + 1) * piece)
        copy = pltpu.make_async_copy(
            solved_ref.at[column, rows], out_ref.at[rows, column * block : (column + 1) * block],
            out_sem.at[column, part],
        )
        copy.start()
        written.append(copy)

    def use_stages(arrive, feed):
        stages = stages_of(blocks)
        totals, started = {}, {}

        def begin(n):
            part_ref, inbox_ref, _, *sems = rest[7 * n : 7 * n + 7]
            arrive(stages[n])
            gram_rows(stages[n], snapshot_ref, part_ref)
            started[n] = scatter_over_range(part_ref, inbox_ref, *sems[:2])
            feed()

        def middle(n):
            part_ref, inbox_ref, total_ref, *sems = rest[7 * n : 7 * n + 7]
            totals[n] = gather_over_range(
                started[n], part_ref, inbox_ref, total_ref, *sems[2:]
            )
            feed()

        def factor(n, numbers):
            for number in numbers:
                at = sum(b + 1 for b in stages[n] if b < number) * block
                factor_row(
                    number, at, number == blocks - 1, total_gates, rest[7 * n + 2], snapshot_ref,
                    solved_ref, inverse_ref, work_ref, emit,
                )

        def landed(n):
            for copy in totals[n]:
                copy.wait_recv()

        begin(0)
        middle(0)
        for n in range(1, len(stages)):
            begin(n)
            landed(n - 1)
            factor(n - 1, stages[n - 1][:1])
            middle(n)
            factor(n - 1, stages[n - 1][1:])
        landed(len(stages) - 1)
        factor(len(stages) - 1, stages[-1])
        for n in started:
            summed.extend(started[n] + totals[n])

    sent = exchange(
        samples_ref, taps_ref, taper_ref, load, load_const, const_ref, snapshot_ref, low_ref,
        high_ref, padded_ref, outgoing_ref, gathered_ref, stage_ref, spread_ref, group, pulse_sems,
        use_stages,
    )
    for copy in sent + summed:
        copy.wait_send()
    for copy in written:
        copy.wait()


def local(samples, taps, taper):
    gates, width = samples.shape
    tap_count = taps.shape[0]
    half = tap_count // 2
    bins = taper.shape[0]
    devices, ranges = lax.axis_size("pulse"), lax.axis_size("range")
    group = width // bins
    share = gates // devices
    count = share // CHUNKS
    blocks = width // LANES
    cosine, sine, table = doppler_constants(bins * devices, devices, group)
    given = np.concatenate([table, cosine, sine], axis=0)
    dma = pltpu.SemaphoreType.DMA
    own = [
        pltpu.VMEM((blocks, gates, LANES), jnp.float32),
        pltpu.VMEM((half, width), jnp.float32),
        pltpu.VMEM((half, width), jnp.float32),
        pltpu.VMEM((gates + 2 * half, width), jnp.float32),
        pltpu.VMEM((gates, width), jnp.float32),
        pltpu.VMEM((devices, share, width), jnp.float32),
        pltpu.VMEM((devices * count, width), jnp.float32),
        pltpu.VMEM((devices, blocks, share, LANES), jnp.float32),
        pltpu.VMEM(given.shape, jnp.float32),
        pltpu.VMEM((LANES, 2 * LANES), jnp.float32),
        pltpu.VMEM((blocks, gates, LANES), jnp.float32),
        pltpu.VMEM((width, width), jnp.float32),
    ]
    pulse_sems = (
        [dma, dma, dma((blocks, CHUNKS)), dma((2,)), dma((2,))]
        + [dma((devices - 1, CHUNKS))] * 2
        + [dma((devices - 1, blocks, max(CHUNKS, FEEDS)))] * 2
    )
    sums = []
    for stage in stages_of(blocks):
        chunk = slice_rows(sum(b + 1 for b in stage) * LANES, ranges)
        sums += [
            pltpu.VMEM((ranges * chunk, LANES), jnp.float32),
            pltpu.VMEM((ranges - 1, chunk, LANES), jnp.float32),
            pltpu.VMEM((ranges * chunk, LANES), jnp.float32),
        ] + [dma((ranges - 1,))] * 4
    return pl.pallas_call(
        functools.partial(whole_kernel, gates * ranges, group),
        out_shape=jax.ShapeDtypeStruct(samples.shape, jnp.float32),
        in_specs=[
            pl.BlockSpec(memory_space=pl.ANY),
            pl.BlockSpec(memory_space=pltpu.VMEM),
            pl.BlockSpec(memory_space=pltpu.SMEM),
            pl.BlockSpec(memory_space=pl.ANY),
        ],
        out_specs=pl.BlockSpec(memory_space=pl.ANY),
        scratch_shapes=own + pulse_sems + sums,
        compiler_params=pltpu.CompilerParams(
            vmem_limit_bytes=60 << 20, collective_id=1, has_side_effects=True
        ),
        name="whiten",
    )(samples, taps[None, :], taper, given)


def solution(mesh):
    placed = (P("range", "pulse"), P(), P("pulse"))
    return jax.shard_map(
        local, mesh=mesh, in_specs=placed, out_specs=P("range", "pulse"), check_vma=False
    )
```

```python
import functools
import math

import jax
import jax.numpy as jnp
import numpy as np
from jax import lax
from jax.experimental import pallas as pl
from jax.experimental.pallas import tpu as pltpu
from jax.sharding import PartitionSpec as P

LOADING = 0.05


PANEL = 16
LANES = 128
CHUNKS = 4
FEEDS = 2
HIGHEST = lax.Precision.HIGHEST


def split3(x):
    high = x.astype(jnp.bfloat16)
    rest = x - high.astype(jnp.float32)
    middle = rest.astype(jnp.bfloat16)
    low = (rest - middle.astype(jnp.float32)).astype(jnp.bfloat16)
    return high, middle, low


def eliminate_panel(work_ref, first, block):
    last = first + PANEL
    tile = work_ref[first:last, :]
    width = tile.shape[1]
    row = lax.broadcasted_iota(jnp.int32, (PANEL, block), 0)
    columns = [
        jnp.broadcast_to(tile[:, first + c : first + c + 1], (PANEL, block)) for c in range(PANEL)
    ]
    left, right = tile[:, :block], tile[:, block:]
    for r in range(PANEL):
        inverse = lax.rsqrt(columns[r][r : r + 1, :])
        below = jnp.where(row > r, columns[r] * inverse, 0.0)
        for c in range(r + 1, PANEL):
            columns[c] = columns[c] - below * (columns[c][r : r + 1, :] * inverse)
        left_row = left[r : r + 1, :] * inverse
        right_row = right[r : r + 1, :] * inverse
        left = jnp.where(row == r, left_row, left - below * left_row)
        right = jnp.where(row == r, right_row, right - below * right_row)
    tile = jnp.concatenate([left, right], axis=1)
    work_ref[first:last, :] = tile
    if last < block:
        high, middle, low = split3(tile)
        lhs = jnp.concatenate([high, high, middle, middle, high, low], axis=0)[:, :block]
        rhs = jnp.concatenate([high, middle, high, middle, low, high], axis=0)
        update = lax.dot_general(
            lhs, rhs, (((0,), (0,)), ((), ())), preferred_element_type=jnp.float32
        )
        work_ref[last:, :] = work_ref[last:, :] - update[last:, :]


def greet(partners):
    barrier = pltpu.get_barrier_semaphore()
    for axis, target in partners:
        pl.semaphore_signal(
            barrier, inc=1, device_id={axis: target}, device_id_type=pl.DeviceIdType.MESH
        )
    pl.semaphore_wait(barrier, len(partners))


def send(src, dst, send_sem, recv_sem, axis, target):
    copy = pltpu.make_async_remote_copy(
        src_ref=src, dst_ref=dst, send_sem=send_sem, recv_sem=recv_sem,
        device_id={axis: target}, device_id_type=pl.DeviceIdType.MESH,
    )
    copy.start()
    return copy


def slice_rows(rows, ranges):
    return -(-rows // (8 * ranges)) * 8


def stages_of(blocks):
    first = max(blocks // 2, 1)
    return [list(range(first))] + [[b] for b in range(first, blocks)]


def owned_rows(owner, chunk):
    return pl.ds(pl.multiple_of(owner * chunk, 8), chunk)


def scatter_over_range(part_ref, inbox_ref, send_sem, recv_sem):
    me, ranges = lax.axis_index("range"), lax.axis_size("range")
    outs = []
    for shift in range(1, ranges):
        to = lax.rem(me + shift, ranges)
        outs.append(
            send(
                part_ref.at[owned_rows(to, inbox_ref.shape[1])], inbox_ref.at[shift - 1],
                send_sem.at[shift - 1], recv_sem.at[shift - 1], "range", to,
            )
        )
    return outs


def gather_over_range(outs, part_ref, inbox_ref, total_ref, send_sem, recv_sem):
    me, ranges = lax.axis_index("range"), lax.axis_size("range")
    rows = owned_rows(me, inbox_ref.shape[1])
    own = part_ref[rows]
    for shift in range(1, ranges):
        outs[shift - 1].wait_recv()
        own = own + inbox_ref[shift - 1]
    total_ref[rows] = own
    source = total_ref.at[rows]
    return [
        send(
            source, source, send_sem.at[s - 1], recv_sem.at[s - 1],
            "range", lax.rem(me + s, ranges),
        )
        for s in range(1, ranges)
    ]


def dot_nt(x, y):
    return lax.dot_general(
        x, y, (((1,), (1,)), ((), ())), precision=HIGHEST, preferred_element_type=jnp.float32
    )


def gram_rows(stage, snapshot_ref, part_ref):
    block = snapshot_ref.shape[2]
    used = 0
    for number in stage:
        mine = snapshot_ref[number]
        for first in range(0, number + 1, 2):
            blocks = range(first, min(first + 2, number + 1))
            other = jnp.concatenate([snapshot_ref[b] for b in blocks], axis=1)
            gram = lax.dot_general(
                mine, other, (((0,), (0,)), ((), ())), precision=HIGHEST,
                preferred_element_type=jnp.float32,
            )
            for n in range(len(blocks)):
                part_ref[used : used + block, :] = gram[:, n * block : (n + 1) * block]
                used += block
    if part_ref.shape[0] > used:
        part_ref[used:, :] = jnp.zeros((part_ref.shape[0] - used, block), jnp.float32)


def factor_row(
    number, at, last, total_gates, total_ref, snapshot_ref, solved_ref, inverse_ref, work_ref
):
    block = work_ref.shape[0]
    r = lax.broadcasted_iota(jnp.int32, (block, block), 0)
    c = lax.broadcasted_iota(jnp.int32, (block, block), 1)
    piece = snapshot_ref.shape[1] // CHUNKS
    done = number * block
    own = slice(done, done + block)

    def total(b):
        return total_ref[at + b * block : at + (b + 1) * block, :] * (1.0 / total_gates)

    diagonal = total(number) + jnp.where(r == c, LOADING, 0.0)
    left = None
    if number:
        row = jnp.concatenate([total(b) for b in range(number)], axis=1)
        left = dot_nt(row, inverse_ref[:done, :done])
        diagonal = diagonal - dot_nt(left, left)
    work_ref[:, :block] = diagonal
    work_ref[:, block:] = jnp.where(r == c, 1.0, 0.0)

    def subtract(part):
        rows = slice(part * piece, (part + 1) * piece)
        solved_ref[rows, own] = snapshot_ref[number, rows] - dot_nt(solved_ref[rows, :done], left)

    waiting = list(range(CHUNKS)) if number else []
    for step, first in enumerate(range(0, block, PANEL)):
        eliminate_panel(work_ref, first, block)
        if waiting and step % 2 == 0:
            subtract(waiting.pop(0))
    while waiting:
        subtract(waiting.pop(0))
    inverse = work_ref[:, block:]
    for part in range(CHUNKS):
        rows = slice(part * piece, (part + 1) * piece)
        source = solved_ref[rows, own] if number else snapshot_ref[number, rows]
        solved_ref[rows, own] = dot_nt(source, inverse)
    if not last:
        end = done + block
        if number:
            scaled = jnp.dot(inverse, left, precision=HIGHEST, preferred_element_type=jnp.float32)
            inverse_ref[done:end, :done] = -jnp.dot(
                scaled, inverse_ref[:done, :done], precision=HIGHEST,
                preferred_element_type=jnp.float32,
            )
            inverse_ref[:done, done:end] = jnp.zeros((done, block), jnp.float32)
        inverse_ref[done:end, done:end] = inverse


def quarter_turn(x):
    lane = lax.broadcasted_iota(jnp.int32, x.shape, 1)
    width = x.shape[1]
    return jnp.where(
        lane % 2 == 0, pltpu.roll(x, width - 1, axis=1), -pltpu.roll(x, 1, axis=1)
    )


def doppler_constants(pulses, devices, group):
    bins = pulses // devices
    lane = np.arange(bins * group)
    turn = (lane // group)[None, :] * np.arange(devices)[:, None] % pulses
    angle = turn * (2.0 * math.pi / pulses)
    first = np.arange(bins)
    phase = (first[:, None] * first[None, :] % bins) * (2.0 * math.pi / bins)
    cosine, sine = np.cos(phase), np.sin(phase)
    pair = np.stack(
        [np.stack([cosine, -sine], axis=-1), np.stack([sine, cosine], axis=-1)], axis=1
    ) / math.sqrt(pulses)
    table = np.einsum("paqb,cd->pcaqdb", pair, np.eye(group // 2))
    table = table.reshape(bins * group, bins * group)
    return tuple(np.asarray(v, np.float32) for v in (np.cos(angle), np.sin(angle), table))


def transform_chunk(rows, group, gathered_ref, const_ref, stage_ref, spread_ref):
    devices, _, width = gathered_ref.shape
    count = rows.size
    bins = width // group
    for at in range(0, width, LANES):
        lanes = slice(at, at + LANES)
        parts = [gathered_ref[z, rows, lanes] for z in range(devices)]
        turned = [quarter_turn(x) for x in parts]
        for k in range(devices):
            total = None
            for z in range(devices):
                step = z * k % devices
                for weight, term in (
                    (math.cos(2.0 * math.pi * step / devices), parts[z]),
                    (math.sin(2.0 * math.pi * step / devices), turned[z]),
                ):
                    if abs(weight) < 1e-9:
                        continue
                    sign = 1.0 if weight > 0 else -1.0
                    if abs(abs(weight) - 1.0) > 1e-9:
                        term, sign = term * weight, 1.0
                    if total is None:
                        total = term if sign > 0 else -term
                    else:
                        total = total + term if sign > 0 else total - term
            total = total * const_ref[width + k : width + k + 1, lanes] + quarter_turn(
                total
            ) * const_ref[width + devices + k : width + devices + k + 1, lanes]
            stage_ref[k * count : (k + 1) * count, lanes] = total
    mixed = jnp.dot(
        stage_ref[...], const_ref[:width, :], precision=HIGHEST, preferred_element_type=jnp.float32
    )
    place = lax.broadcasted_iota(jnp.int32, (count, LANES), 1) // group
    for target in range(devices):
        for at in range(0, width, LANES):
            out = None
            for n in range(LANES // group):
                k = target * bins + at // group + n
                low, high = k % devices, k // devices
                source = high * group
                block = source // LANES * LANES
                piece = mixed[low * count : (low + 1) * count, block : block + LANES]
                shift = (n * group - source) % LANES
                if shift:
                    piece = pltpu.roll(piece, shift, axis=1)
                out = piece if out is None else jnp.where(place == n, piece, out)
            spread_ref[target, at // LANES, rows, :] = out


def exchange(
    samples_ref, taps_ref, taper_ref, load, load_const, const_ref, snapshot_ref, low_ref, high_ref,
    padded_ref, outgoing_ref, gathered_ref, stage_ref, spread_ref, group, sems, use_stages
):
    halo_send, halo_recv, in_send, in_recv, back_send, back_recv = sems
    gates, width = samples_ref.shape
    devices, share, _ = gathered_ref.shape
    half = low_ref.shape[0]
    count = share // CHUNKS
    z = lax.axis_index("pulse")
    me, ranges = lax.axis_index("range"), lax.axis_size("range")

    halos = [
        send(
            samples_ref.at[gates - half :], low_ref, halo_send.at[0], halo_recv.at[0],
            "range", lax.rem(me + 1, ranges),
        ),
        send(
            samples_ref.at[:half], high_ref, halo_send.at[1], halo_recv.at[1],
            "range", lax.rem(me + ranges - 1, ranges),
        ),
    ]
    tap_count = taps_ref.shape[1]
    room = -(-(tap_count + count) // LANES) * LANES
    taps = jnp.concatenate(
        [taps_ref[...], jnp.zeros((1, room - tap_count), jnp.float32)], axis=1
    )
    span = count + 2 * half
    band = pltpu.roll(
        jnp.broadcast_to(taps, (count, room)), 0, axis=1, stride=1, stride_axis=0
    )[:, :span]
    pulse = lax.broadcasted_iota(jnp.int32, (1, width), 1) // group
    taper = jnp.zeros((1, width), jnp.float32)
    for p in range(width // group):
        taper = jnp.where(pulse == p, taper_ref[p], taper)
    inner = [
        p for p in range(CHUNKS) if p * count >= half and share - (p + 1) * count >= half
    ]
    outer = [p for p in range(CHUNKS) if p not in inner]
    order = inner + outer
    shifts = sorted(range(1, devices), key=lambda s: abs(2 * s - devices))
    ins = {}
    load.wait()
    for part in order:
        if part == outer[0]:
            for copy in halos:
                copy.wait_recv()
            padded_ref[:half, :] = jnp.where(me > 0, low_ref[...], 0.0)
            padded_ref[half + gates :, :] = jnp.where(me < ranges - 1, high_ref[...], 0.0)
        for shift in shifts + [0]:
            target = lax.rem(z + shift, devices)
            start = pl.multiple_of(target * share + part * count, 8)
            value = taper * jnp.dot(
                band, padded_ref[pl.ds(start, span), :], precision=HIGHEST,
                preferred_element_type=jnp.float32,
            )
            rows = pl.ds(part * count, count)
            if shift == 0:
                gathered_ref[z, rows, :] = value
                continue
            here = outgoing_ref.at[pl.ds(start, count)]
            here[...] = value
            ins[part, shift] = send(
                here, gathered_ref.at[z, rows], in_send.at[shift - 1, part],
                in_recv.at[shift - 1, part], "pulse", target,
            )
    load_const.wait()
    backs = {}
    blocks = width // LANES
    early = len(stages_of(blocks)[0])
    length = share // FEEDS
    later = [(b, n, n * length, length) for b in range(early, blocks) for n in range(FEEDS)]

    def feed():
        if later:
            send_back(*later.pop(0))

    def arrive(stage):
        while later and later[0][0] in stage:
            feed()
        for block in stage:
            for copy in backs[block]:
                copy.wait_recv()

    def send_back(block, part, start, length):
        for shift in shifts:
            target = lax.rem(z + shift, devices)
            home = pl.ds(pl.multiple_of(z * share + start, 8), length)
            backs.setdefault(block, []).append(
                send(
                    spread_ref.at[target, block, pl.ds(start, length)],
                    snapshot_ref.at[block, home],
                    back_send.at[shift - 1, block, part], back_recv.at[shift - 1, block, part],
                    "pulse", target,
                )
            )

    for part in order:
        rows = pl.ds(part * count, count)
        for shift in shifts:
            ins[part, shift].wait_recv()
        transform_chunk(rows, group, gathered_ref, const_ref, stage_ref, spread_ref)
        for block in range(early):
            send_back(block, part, part * count, count)
        home = pl.ds(pl.multiple_of(z * share + part * count, 8), count)
        for block in range(blocks):
            snapshot_ref[block, home, :] = spread_ref[z, block, rows, :]
    feed()
    use_stages(arrive, feed)
    return halos + list(ins.values()) + [copy for b in range(blocks) for copy in backs[b]]


def whole_kernel(
    total_gates, group, samples_ref, taps_ref, taper_ref, given_ref, solved_ref,
    snapshot_ref, low_ref, high_ref, padded_ref, outgoing_ref, gathered_ref, stage_ref,
    spread_ref, const_ref, work_ref, inverse_ref, load_sem, const_sem, *rest
):
    z, devices = lax.axis_index("pulse"), lax.axis_size("pulse")
    me, ranges = lax.axis_index("range"), lax.axis_size("range")
    gates, width = samples_ref.shape
    blocks, _, block = snapshot_ref.shape
    half = low_ref.shape[0]
    pulse_sems, rest = rest[:6], rest[6:]
    load = pltpu.make_async_copy(samples_ref, padded_ref.at[half : half + gates], load_sem)
    load.start()
    load_const = pltpu.make_async_copy(given_ref, const_ref, const_sem)
    load_const.start()
    greet(
        [("range", lax.rem(me + shift, ranges)) for shift in range(1, ranges)]
        + [("pulse", lax.rem(z + shift, devices)) for shift in range(1, devices)]
    )
    summed = []

    def use_stages(arrive, feed):
        stages = stages_of(blocks)
        totals, started = {}, {}

        def begin(n):
            part_ref, inbox_ref, _, *sems = rest[7 * n : 7 * n + 7]
            arrive(stages[n])
            gram_rows(stages[n], snapshot_ref, part_ref)
            started[n] = scatter_over_range(part_ref, inbox_ref, *sems[:2])
            feed()

        def middle(n):
            part_ref, inbox_ref, total_ref, *sems = rest[7 * n : 7 * n + 7]
            totals[n] = gather_over_range(
                started[n], part_ref, inbox_ref, total_ref, *sems[2:]
            )
            feed()

        def factor(n, number):
            at = sum(b + 1 for b in stages[n] if b < number) * block
            factor_row(
                number, at, number == blocks - 1, total_gates, rest[7 * n + 2], snapshot_ref,
                solved_ref, inverse_ref, work_ref,
            )

        def landed(n):
            for copy in totals[n]:
                copy.wait_recv()

        begin(0)
        middle(0)
        ready = []
        for n in range(1, len(stages)):
            begin(n)
            if not ready:
                landed(n - 1)
                ready = [(n - 1, number) for number in stages[n - 1]]
            factor(*ready.pop(0))
            middle(n)
            if n > 1:
                while ready:
                    factor(*ready.pop(0))
                landed(n - 1)
                ready = [(n - 1, number) for number in stages[n - 1]]
        while ready:
            factor(*ready.pop(0))
        landed(len(stages) - 1)
        for number in stages[-1]:
            factor(len(stages) - 1, number)
        for n in started:
            summed.extend(started[n] + totals[n])

    sent = exchange(
        samples_ref, taps_ref, taper_ref, load, load_const, const_ref, snapshot_ref, low_ref,
        high_ref, padded_ref, outgoing_ref, gathered_ref, stage_ref, spread_ref, group, pulse_sems,
        use_stages,
    )
    for copy in sent + summed:
        copy.wait_send()


def local(samples, taps, taper):
    gates, width = samples.shape
    tap_count = taps.shape[0]
    half = tap_count // 2
    bins = taper.shape[0]
    devices, ranges = lax.axis_size("pulse"), lax.axis_size("range")
    group = width // bins
    share = gates // devices
    count = share // CHUNKS
    blocks = width // LANES
    cosine, sine, table = doppler_constants(bins * devices, devices, group)
    given = np.concatenate([table, cosine, sine], axis=0)
    dma = pltpu.SemaphoreType.DMA
    own = [
        pltpu.VMEM((blocks, gates, LANES), jnp.float32),
        pltpu.VMEM((half, width), jnp.float32),
        pltpu.VMEM((half, width), jnp.float32),
        pltpu.VMEM((gates + 2 * half, width), jnp.float32),
        pltpu.VMEM((gates, width), jnp.float32),
        pltpu.VMEM((devices, share, width), jnp.float32),
        pltpu.VMEM((devices * count, width), jnp.float32),
        pltpu.VMEM((devices, blocks, share, LANES), jnp.float32),
        pltpu.VMEM(given.shape, jnp.float32),
        pltpu.VMEM((LANES, 2 * LANES), jnp.float32),
        pltpu.VMEM((width, width), jnp.float32),
    ]
    pulse_sems = (
        [dma, dma, dma((2,)), dma((2,))]
        + [dma((devices - 1, CHUNKS))] * 2
        + [dma((devices - 1, blocks, max(CHUNKS, FEEDS)))] * 2
    )
    sums = []
    for stage in stages_of(blocks):
        chunk = slice_rows(sum(b + 1 for b in stage) * LANES, ranges)
        sums += [
            pltpu.VMEM((ranges * chunk, LANES), jnp.float32),
            pltpu.VMEM((ranges - 1, chunk, LANES), jnp.float32),
            pltpu.VMEM((ranges * chunk, LANES), jnp.float32),
        ] + [dma((ranges - 1,))] * 4
    return pl.pallas_call(
        functools.partial(whole_kernel, gates * ranges, group),
        out_shape=pltpu.VMEM(samples.shape, jnp.float32),
        in_specs=[
            pl.BlockSpec(memory_space=pl.ANY),
            pl.BlockSpec(memory_space=pltpu.VMEM),
            pl.BlockSpec(memory_space=pltpu.SMEM),
            pl.BlockSpec(memory_space=pl.ANY),
        ],
        out_specs=pl.BlockSpec(memory_space=pltpu.VMEM),
        scratch_shapes=own + pulse_sems + sums,
        compiler_params=pltpu.CompilerParams(
            vmem_limit_bytes=61 << 20, collective_id=1, has_side_effects=True
        ),
        name="whiten",
    )(samples, taps[None, :], taper, given)


def solution(mesh):
    placed = (P("range", "pulse"), P(), P("pulse"))
    return jax.shard_map(
        local, mesh=mesh, in_specs=placed, out_specs=P("range", "pulse"), check_vma=False
    )
```

```python
import functools
import math

import jax
import jax.numpy as jnp
import numpy as np
from jax import lax
from jax.experimental import pallas as pl
from jax.experimental.pallas import tpu as pltpu
from jax.sharding import PartitionSpec as P

LOADING = 0.05


PANEL = 16
LANES = 128
CHUNKS = 4
FEEDS = 2
HIGHEST = lax.Precision.HIGHEST


def split3(x):
    high = x.astype(jnp.bfloat16)
    rest = x - high.astype(jnp.float32)
    middle = rest.astype(jnp.bfloat16)
    low = (rest - middle.astype(jnp.float32)).astype(jnp.bfloat16)
    return high, middle, low


def split2(x):
    high = x.astype(jnp.bfloat16)
    return high, (x - high.astype(jnp.float32)).astype(jnp.bfloat16)


def eliminate_panel(work_ref, first, block):
    last = first + PANEL
    tile = work_ref[first:last, :]
    width = tile.shape[1]
    row = lax.broadcasted_iota(jnp.int32, (PANEL, block), 0)
    columns = [
        jnp.broadcast_to(tile[:, first + c : first + c + 1], (PANEL, block)) for c in range(PANEL)
    ]
    left, right = tile[:, :block], tile[:, block:]
    for r in range(PANEL):
        inverse = lax.rsqrt(columns[r][r : r + 1, :])
        below = jnp.where(row > r, columns[r] * inverse, 0.0)
        for c in range(r + 1, PANEL):
            columns[c] = columns[c] - below * (columns[c][r : r + 1, :] * inverse)
        left_row = left[r : r + 1, :] * inverse
        right_row = right[r : r + 1, :] * inverse
        left = jnp.where(row == r, left_row, left - below * left_row)
        right = jnp.where(row == r, right_row, right - below * right_row)
    tile = jnp.concatenate([left, right], axis=1)
    work_ref[first:last, :] = tile
    if last < block:
        high, middle, low = split3(tile)
        lhs = jnp.concatenate([high, high, middle, middle, high, low], axis=0)[:, :block]
        rhs = jnp.concatenate([high, middle, high, middle, low, high], axis=0)
        update = lax.dot_general(
            lhs, rhs, (((0,), (0,)), ((), ())), preferred_element_type=jnp.float32
        )
        work_ref[last:, :] = work_ref[last:, :] - update[last:, :]


def greet(partners):
    barrier = pltpu.get_barrier_semaphore()
    for axis, target in partners:
        pl.semaphore_signal(
            barrier, inc=1, device_id={axis: target}, device_id_type=pl.DeviceIdType.MESH
        )
    pl.semaphore_wait(barrier, len(partners))


def send(src, dst, send_sem, recv_sem, axis, target):
    copy = pltpu.make_async_remote_copy(
        src_ref=src, dst_ref=dst, send_sem=send_sem, recv_sem=recv_sem,
        device_id={axis: target}, device_id_type=pl.DeviceIdType.MESH,
    )
    copy.start()
    return copy


def slice_rows(rows, ranges):
    return -(-rows // (8 * ranges)) * 8


def stages_of(blocks):
    first = 1
    return [list(range(first))] + [[b] for b in range(first, blocks)]


def owned_rows(owner, chunk):
    return pl.ds(pl.multiple_of(owner * chunk, 8), chunk)


def scatter_over_range(part_ref, inbox_ref, send_sem, recv_sem):
    me, ranges = lax.axis_index("range"), lax.axis_size("range")
    outs = []
    for shift in range(1, ranges):
        to = lax.rem(me + shift, ranges)
        outs.append(
            send(
                part_ref.at[owned_rows(to, inbox_ref.shape[1])], inbox_ref.at[shift - 1],
                send_sem.at[shift - 1], recv_sem.at[shift - 1], "range", to,
            )
        )
    return outs


def gather_over_range(outs, part_ref, inbox_ref, total_ref, send_sem, recv_sem):
    me, ranges = lax.axis_index("range"), lax.axis_size("range")
    rows = owned_rows(me, inbox_ref.shape[1])
    own = part_ref[rows]
    for shift in range(1, ranges):
        outs[shift - 1].wait_recv()
        own = own + inbox_ref[shift - 1]
    total_ref[rows] = own
    source = total_ref.at[rows]
    return [
        send(
            source, source, send_sem.at[s - 1], recv_sem.at[s - 1],
            "range", lax.rem(me + s, ranges),
        )
        for s in range(1, ranges)
    ]


def dot_nt(x, y):
    return lax.dot_general(
        x, y, (((1,), (1,)), ((), ())), precision=HIGHEST, preferred_element_type=jnp.float32
    )


def gram_rows(stage, snapshot_ref, part_ref):
    block = snapshot_ref.shape[2]
    used = 0
    for number in stage:
        high, low = split2(snapshot_ref[number])
        mine = jnp.concatenate([high, high, low, low], axis=0)
        for first in range(0, number + 1, 2):
            blocks = range(first, min(first + 2, number + 1))
            high, low = split2(jnp.concatenate([snapshot_ref[b] for b in blocks], axis=1))
            gram = lax.dot_general(
                mine, jnp.concatenate([high, low, high, low], axis=0), (((0,), (0,)), ((), ())),
                preferred_element_type=jnp.float32,
            )
            for n in range(len(blocks)):
                part_ref[used : used + block, :] = gram[:, n * block : (n + 1) * block]
                used += block
    if part_ref.shape[0] > used:
        part_ref[used:, :] = jnp.zeros((part_ref.shape[0] - used, block), jnp.float32)


def factor_row(
    number, at, last, total_gates, total_ref, snapshot_ref, solved_ref, inverse_ref, work_ref
):
    block = work_ref.shape[0]
    r = lax.broadcasted_iota(jnp.int32, (block, block), 0)
    c = lax.broadcasted_iota(jnp.int32, (block, block), 1)
    piece = snapshot_ref.shape[1] // CHUNKS
    done = number * block
    own = slice(done, done + block)

    def total(b):
        return total_ref[at + b * block : at + (b + 1) * block, :] * (1.0 / total_gates)

    diagonal = total(number) + jnp.where(r == c, LOADING, 0.0)
    left = None
    if number:
        row = jnp.concatenate([total(b) for b in range(number)], axis=1)
        left = dot_nt(row, inverse_ref[:done, :done])
        diagonal = diagonal - dot_nt(left, left)
    work_ref[:, :block] = diagonal
    work_ref[:, block:] = jnp.where(r == c, 1.0, 0.0)

    def subtract(part):
        rows = slice(part * piece, (part + 1) * piece)
        solved_ref[rows, own] = snapshot_ref[number, rows] - dot_nt(solved_ref[rows, :done], left)

    waiting = list(range(CHUNKS)) if number else []
    for step, first in enumerate(range(0, block, PANEL)):
        eliminate_panel(work_ref, first, block)
        if waiting and step % 2 == 0:
            subtract(waiting.pop(0))
    while waiting:
        subtract(waiting.pop(0))
    inverse = work_ref[:, block:]
    for part in range(CHUNKS):
        rows = slice(part * piece, (part + 1) * piece)
        source = solved_ref[rows, own] if number else snapshot_ref[number, rows]
        solved_ref[rows, own] = dot_nt(source, inverse)
    if not last:
        end = done + block
        if number:
            scaled = jnp.dot(inverse, left, precision=HIGHEST, preferred_element_type=jnp.float32)
            inverse_ref[done:end, :done] = -jnp.dot(
                scaled, inverse_ref[:done, :done], precision=HIGHEST,
                preferred_element_type=jnp.float32,
            )
            inverse_ref[:done, done:end] = jnp.zeros((done, block), jnp.float32)
        inverse_ref[done:end, done:end] = inverse


def quarter_turn(x):
    lane = lax.broadcasted_iota(jnp.int32, x.shape, 1)
    width = x.shape[1]
    return jnp.where(
        lane % 2 == 0, pltpu.roll(x, width - 1, axis=1), -pltpu.roll(x, 1, axis=1)
    )


def doppler_constants(pulses, devices, group):
    bins = pulses // devices
    lane = np.arange(bins * group)
    turn = (lane // group)[None, :] * np.arange(devices)[:, None] % pulses
    angle = turn * (2.0 * math.pi / pulses)
    first = np.arange(bins)
    phase = (first[:, None] * first[None, :] % bins) * (2.0 * math.pi / bins)
    cosine, sine = np.cos(phase), np.sin(phase)
    pair = np.stack(
        [np.stack([cosine, -sine], axis=-1), np.stack([sine, cosine], axis=-1)], axis=1
    ) / math.sqrt(pulses)
    table = np.einsum("paqb,cd->pcaqdb", pair, np.eye(group // 2))
    table = table.reshape(bins * group, bins * group)
    return tuple(np.asarray(v, np.float32) for v in (np.cos(angle), np.sin(angle), table))


def transform_chunk(rows, group, gathered_ref, const_ref, stage_ref, spread_ref):
    devices, _, width = gathered_ref.shape
    count = rows.size
    bins = width // group
    for at in range(0, width, LANES):
        lanes = slice(at, at + LANES)
        parts = [gathered_ref[z, rows, lanes] for z in range(devices)]
        turned = [quarter_turn(x) for x in parts]
        for k in range(devices):
            total = None
            for z in range(devices):
                step = z * k % devices
                for weight, term in (
                    (math.cos(2.0 * math.pi * step / devices), parts[z]),
                    (math.sin(2.0 * math.pi * step / devices), turned[z]),
                ):
                    if abs(weight) < 1e-9:
                        continue
                    sign = 1.0 if weight > 0 else -1.0
                    if abs(abs(weight) - 1.0) > 1e-9:
                        term, sign = term * weight, 1.0
                    if total is None:
                        total = term if sign > 0 else -term
                    else:
                        total = total + term if sign > 0 else total - term
            total = total * const_ref[width + k : width + k + 1, lanes] + quarter_turn(
                total
            ) * const_ref[width + devices + k : width + devices + k + 1, lanes]
            stage_ref[k * count : (k + 1) * count, lanes] = total
    mixed = jnp.dot(
        stage_ref[...], const_ref[:width, :], precision=HIGHEST, preferred_element_type=jnp.float32
    )
    place = lax.broadcasted_iota(jnp.int32, (count, LANES), 1) // group
    for target in range(devices):
        for at in range(0, width, LANES):
            out = None
            for n in range(LANES // group):
                k = target * bins + at // group + n
                low, high = k % devices, k // devices
                source = high * group
                block = source // LANES * LANES
                piece = mixed[low * count : (low + 1) * count, block : block + LANES]
                shift = (n * group - source) % LANES
                if shift:
                    piece = pltpu.roll(piece, shift, axis=1)
                out = piece if out is None else jnp.where(place == n, piece, out)
            spread_ref[target, at // LANES, rows, :] = out


def exchange(
    samples_ref, taps_ref, taper_ref, load, load_const, const_ref, snapshot_ref, low_ref, high_ref,
    padded_ref, outgoing_ref, gathered_ref, stage_ref, spread_ref, group, sems, use_stages
):
    halo_send, halo_recv, in_send, in_recv, back_send, back_recv = sems
    gates, width = samples_ref.shape
    devices, share, _ = gathered_ref.shape
    half = low_ref.shape[0]
    count = share // CHUNKS
    z = lax.axis_index("pulse")
    me, ranges = lax.axis_index("range"), lax.axis_size("range")

    halos = [
        send(
            samples_ref.at[gates - half :], low_ref, halo_send.at[0], halo_recv.at[0],
            "range", lax.rem(me + 1, ranges),
        ),
        send(
            samples_ref.at[:half], high_ref, halo_send.at[1], halo_recv.at[1],
            "range", lax.rem(me + ranges - 1, ranges),
        ),
    ]
    tap_count = taps_ref.shape[1]
    room = -(-(tap_count + count) // LANES) * LANES
    taps = jnp.concatenate(
        [taps_ref[...], jnp.zeros((1, room - tap_count), jnp.float32)], axis=1
    )
    span = count + 2 * half
    band = pltpu.roll(
        jnp.broadcast_to(taps, (count, room)), 0, axis=1, stride=1, stride_axis=0
    )[:, :span]
    pulse = lax.broadcasted_iota(jnp.int32, (1, width), 1) // group
    taper = jnp.zeros((1, width), jnp.float32)
    for p in range(width // group):
        taper = jnp.where(pulse == p, taper_ref[p], taper)
    inner = [
        p for p in range(CHUNKS) if p * count >= half and share - (p + 1) * count >= half
    ]
    outer = [p for p in range(CHUNKS) if p not in inner]
    order = inner + outer
    shifts = sorted(range(1, devices), key=lambda s: abs(2 * s - devices))
    ins = {}
    load.wait()
    for part in order:
        if part == outer[0]:
            for copy in halos:
                copy.wait_recv()
            padded_ref[:half, :] = jnp.where(me > 0, low_ref[...], 0.0)
            padded_ref[half + gates :, :] = jnp.where(me < ranges - 1, high_ref[...], 0.0)
        for shift in shifts + [0]:
            target = lax.rem(z + shift, devices)
            start = pl.multiple_of(target * share + part * count, 8)
            value = taper * jnp.dot(
                band, padded_ref[pl.ds(start, span), :], precision=HIGHEST,
                preferred_element_type=jnp.float32,
            )
            rows = pl.ds(part * count, count)
            if shift == 0:
                gathered_ref[z, rows, :] = value
                continue
            here = outgoing_ref.at[pl.ds(start, count)]
            here[...] = value
            ins[part, shift] = send(
                here, gathered_ref.at[z, rows], in_send.at[shift - 1, part],
                in_recv.at[shift - 1, part], "pulse", target,
            )
    load_const.wait()
    backs = {}
    blocks = width // LANES
    early = len(stages_of(blocks)[0])
    length = share // FEEDS
    later = [(b, n, n * length, length) for b in range(early, blocks) for n in range(FEEDS)]

    def feed():
        if later:
            send_back(*later.pop(0))

    def arrive(stage):
        while later and later[0][0] in stage:
            feed()
        for block in stage:
            for copy in backs[block]:
                copy.wait_recv()

    def send_back(block, part, start, length):
        for shift in shifts:
            target = lax.rem(z + shift, devices)
            home = pl.ds(pl.multiple_of(z * share + start, 8), length)
            backs.setdefault(block, []).append(
                send(
                    spread_ref.at[target, block, pl.ds(start, length)],
                    snapshot_ref.at[block, home],
                    back_send.at[shift - 1, block, part], back_recv.at[shift - 1, block, part],
                    "pulse", target,
                )
            )

    for part in order:
        rows = pl.ds(part * count, count)
        for shift in shifts:
            ins[part, shift].wait_recv()
        transform_chunk(rows, group, gathered_ref, const_ref, stage_ref, spread_ref)
        for block in range(early):
            send_back(block, part, part * count, count)
        home = pl.ds(pl.multiple_of(z * share + part * count, 8), count)
        for block in range(blocks):
            snapshot_ref[block, home, :] = spread_ref[z, block, rows, :]
    feed()
    use_stages(arrive, feed)
    return halos + list(ins.values()) + [copy for b in range(blocks) for copy in backs[b]]


def whole_kernel(
    total_gates, group, samples_ref, taps_ref, taper_ref, given_ref, solved_ref,
    snapshot_ref, low_ref, high_ref, padded_ref, outgoing_ref, gathered_ref, stage_ref,
    spread_ref, const_ref, work_ref, inverse_ref, load_sem, const_sem, *rest
):
    z, devices = lax.axis_index("pulse"), lax.axis_size("pulse")
    me, ranges = lax.axis_index("range"), lax.axis_size("range")
    gates, width = samples_ref.shape
    blocks, _, block = snapshot_ref.shape
    half = low_ref.shape[0]
    pulse_sems, rest = rest[:6], rest[6:]
    load = pltpu.make_async_copy(samples_ref, padded_ref.at[half : half + gates], load_sem)
    load.start()
    load_const = pltpu.make_async_copy(given_ref, const_ref, const_sem)
    load_const.start()
    greet(
        [("range", lax.rem(me + shift, ranges)) for shift in range(1, ranges)]
        + [("pulse", lax.rem(z + shift, devices)) for shift in range(1, devices)]
    )
    summed = []

    def use_stages(arrive, feed):
        stages = stages_of(blocks)
        totals, started = {}, {}

        def begin(n):
            part_ref, inbox_ref, _, *sems = rest[7 * n : 7 * n + 7]
            arrive(stages[n])
            gram_rows(stages[n], snapshot_ref, part_ref)
            started[n] = scatter_over_range(part_ref, inbox_ref, *sems[:2])
            feed()

        def middle(n):
            part_ref, inbox_ref, total_ref, *sems = rest[7 * n : 7 * n + 7]
            totals[n] = gather_over_range(
                started[n], part_ref, inbox_ref, total_ref, *sems[2:]
            )
            feed()

        def factor(n, number):
            at = sum(b + 1 for b in stages[n] if b < number) * block
            factor_row(
                number, at, number == blocks - 1, total_gates, rest[7 * n + 2], snapshot_ref,
                solved_ref, inverse_ref, work_ref,
            )

        def landed(n):
            for copy in totals[n]:
                copy.wait_recv()

        begin(0)
        middle(0)
        for n in range(1, len(stages)):
            begin(n)
            final = n == len(stages) - 1
            if final:
                middle(n)
            landed(n - 1)
            for number in stages[n - 1]:
                factor(n - 1, number)
            if not final:
                middle(n)
        landed(len(stages) - 1)
        for number in stages[-1]:
            factor(len(stages) - 1, number)
        for n in started:
            summed.extend(started[n] + totals[n])

    sent = exchange(
        samples_ref, taps_ref, taper_ref, load, load_const, const_ref, snapshot_ref, low_ref,
        high_ref, padded_ref, outgoing_ref, gathered_ref, stage_ref, spread_ref, group, pulse_sems,
        use_stages,
    )
    for copy in sent + summed:
        copy.wait_send()


def local(samples, taps, taper):
    gates, width = samples.shape
    tap_count = taps.shape[0]
    half = tap_count // 2
    bins = taper.shape[0]
    devices, ranges = lax.axis_size("pulse"), lax.axis_size("range")
    group = width // bins
    share = gates // devices
    count = share // CHUNKS
    blocks = width // LANES
    cosine, sine, table = doppler_constants(bins * devices, devices, group)
    given = np.concatenate([table, cosine, sine], axis=0)
    dma = pltpu.SemaphoreType.DMA
    own = [
        pltpu.VMEM((blocks, gates, LANES), jnp.float32),
        pltpu.VMEM((half, width), jnp.float32),
        pltpu.VMEM((half, width), jnp.float32),
        pltpu.VMEM((gates + 2 * half, width), jnp.float32),
        pltpu.VMEM((gates, width), jnp.float32),
        pltpu.VMEM((devices, share, width), jnp.float32),
        pltpu.VMEM((devices * count, width), jnp.float32),
        pltpu.VMEM((devices, blocks, share, LANES), jnp.float32),
        pltpu.VMEM(given.shape, jnp.float32),
        pltpu.VMEM((LANES, 2 * LANES), jnp.float32),
        pltpu.VMEM((width, width), jnp.float32),
    ]
    pulse_sems = (
        [dma, dma, dma((2,)), dma((2,))]
        + [dma((devices - 1, CHUNKS))] * 2
        + [dma((devices - 1, blocks, max(CHUNKS, FEEDS)))] * 2
    )
    sums = []
    for stage in stages_of(blocks):
        chunk = slice_rows(sum(b + 1 for b in stage) * LANES, ranges)
        sums += [
            pltpu.VMEM((ranges * chunk, LANES), jnp.float32),
            pltpu.VMEM((ranges - 1, chunk, LANES), jnp.float32),
            pltpu.VMEM((ranges * chunk, LANES), jnp.float32),
        ] + [dma((ranges - 1,))] * 4
    return pl.pallas_call(
        functools.partial(whole_kernel, gates * ranges, group),
        out_shape=pltpu.VMEM(samples.shape, jnp.float32),
        in_specs=[
            pl.BlockSpec(memory_space=pl.ANY),
            pl.BlockSpec(memory_space=pltpu.VMEM),
            pl.BlockSpec(memory_space=pltpu.SMEM),
            pl.BlockSpec(memory_space=pl.ANY),
        ],
        out_specs=pl.BlockSpec(memory_space=pltpu.VMEM),
        scratch_shapes=own + pulse_sems + sums,
        compiler_params=pltpu.CompilerParams(
            vmem_limit_bytes=61 << 20, collective_id=1, has_side_effects=True
        ),
        name="whiten",
    )(samples, taps[None, :], taper, given)


def solution(mesh):
    placed = (P("range", "pulse"), P(), P("pulse"))
    return jax.shard_map(
        local, mesh=mesh, in_specs=placed, out_specs=P("range", "pulse"), check_vma=False
    )
```
